32 devices in a mesh: gx: 2 (over y), gy: 4 (over x, core), gz: 4 (over z).
Axes of the slice: x: 2, y: 2, z: 4, core: 2. Of those that a mesh axis runs over, the one named last changes fastest.
Arguments:
- density: float32 [16, 32, 512], P('gx', 'gy', 'gz'), may hold values from 0.5 to 2
- momentum: float32 [3, 16, 32, 512], P(None, 'gx', 'gy', 'gz'), may hold values from -3 to 3
- energy: float32 [16, 32, 512], P('gx', 'gy', 'gz'), may hold values from 1 to 4
- material: int32 [16, 32, 512], P('gx', 'gy', 'gz'), may hold values from 1 to 7
- tick_counts: int32 [3], replicated, may hold values from 1 to 4
Outputs:
- density_out: float32 [16, 32, 512], P('gx', 'gy', 'gz')
- momentum_out: float32 [3, 16, 32, 512], P(None, 'gx', 'gy', 'gz')
- energy_out: float32 [16, 32, 512], P('gx', 'gy', 'gz')
The draws below stay inside these ranges and needn't reach their ends.
Inputs may be any that keep to these rules, and one draw needn't show every extreme that they name: `material`: bits 1, 2 and 4 say whether water, air and basalt are present in the cell; at least one is.
All inputs are finite; a program needn't handle non-finite values.
Results may differ from the reference program's by a relative error of at most 0.0003.
Values sent between devices are 32-bit elements; how exact they have to be, the bound alone decides.
A program may use at most 64 MiB of HBM per device.

```python
import math
import jax
import jax.numpy as jnp
from jax import lax

STEPS = 3
ITERS = 4
NX = 16
NY = 32
NZ = 512


def set_ends(entries, rng, smallest, largest):
    spot = [jax.random.randint(jax.random.fold_in(rng, axis), (), 0, length) for axis, length in enumerate(entries.shape)]
    widest = entries.shape.index(max(entries.shape))
    neighbour = spot[:widest] + [(spot[widest] + 1) % entries.shape[widest]] + spot[widest + 1:]
    return entries.at[tuple(spot)].set(smallest).at[tuple(neighbour)].set(largest)


def steps_of(key, extent, split, least, top_value):
    def one(position, shards_of):
        heights = jax.random.uniform(jax.random.fold_in(jax.random.fold_in(key, 6), position), (shards_of,), jnp.float32, least / len(split), top_value / len(split))
        return jnp.repeat(jnp.exp(heights), extent[position] // shards_of).reshape((-1,) + (1,) * (len(extent) - position - 1))

    loudness = one(*split[0])
    for cut in split[1:]:
        loudness = loudness * one(*cut)
    return loudness


def centred(stream_key, shape, spread, bound, shards=(), kind=jnp.bfloat16):
    factor_of = steps_of(stream_key, shape, shards, -0.22, 0.18) if shards else 1.0
    result = jax.random.normal(stream_key, shape, jnp.float32) * spread * factor_of
    return jnp.minimum(jnp.maximum(result, -bound), bound).astype(kind)


def setup_inputs(seed: int = 0) -> dict:
    key_of = jax.random.split(jax.random.key(seed), 6)
    return {
        "density": jnp.clip(jnp.exp(math.log(2.0) - 1.3862944 * jax.random.uniform(key_of[0], (NX, NY, NZ), jnp.float32) ** steps_of(key_of[0], (NX, NY, NZ), ((0, 2), (1, 4), (2, 4)), -0.2, 0.2)), 0.5, 2.0),
        "momentum": centred(key_of[1], (3, NX, NY, NZ), 0.5, 3.0, ((1, 2), (2, 4), (3, 4)), jnp.float32),
        "energy": jnp.clip(jnp.exp(math.log(4.0) - 1.3862944 * jax.random.uniform(key_of[2], (NX, NY, NZ), jnp.float32) ** steps_of(key_of[2], (NX, NY, NZ), ((0, 2), (1, 4), (2, 4)), -0.2, 0.2)), 1.0, 4.0),
        "material": set_ends(jax.random.randint(key_of[3], (NX, NY, NZ), 1, 8), jax.random.fold_in(key_of[3], 1), 1, 7).astype(jnp.int32),
        "tick_counts": jax.random.randint(key_of[4], (STEPS,), 1, 5).astype(jnp.int32),
    }


RHO_REF = (1.0, 0.5, 2.7)
BULK_LIN = (1.0, 0.0, 12.0)
BULK_QUAD = (6.0, 0.0, 12.0)
COEF_LOW = (0.7, 0.4, 0.5)
COEF_HIGH = (0.15, 0.0, 1.5)
ENERGY_REF = (3.0, 1.0, 20.0)
TIME_UNIT = 0.015

def smooth_pos(value):
    return 0.5 * (value + jnp.sqrt(value * value + 0.01))

def tillotson(phase, heat, material_id):
    compression = phase / RHO_REF[material_id]
    strain = compression - 1.0
    ratio = heat / (ENERGY_REF[material_id] * compression * compression) + 1.0
    return (COEF_LOW[material_id] + COEF_HIGH[material_id] / ratio) * phase * heat + BULK_LIN[material_id] * strain + BULK_QUAD[material_id] * strain * strain

def sound_sq(heat, material_id):
    return BULK_LIN[material_id] / RHO_REF[material_id] + (COEF_LOW[material_id] + COEF_HIGH[material_id]) * heat + 0.1

def state_eos(conserved, material):
    mixture = smooth_pos(conserved[0])
    velocity = conserved[1:4] / mixture
    heat = smooth_pos(conserved[4] / mixture - 0.5 * lax.optimization_barrier(jnp.sum(velocity * velocity, 0)))
    present = [(material // 2 ** material_id % 2).astype(jnp.float32) for material_id in range(3)]
    present_count = present[0] + present[1] + present[2]
    shares = [flag / present_count for flag in present]
    squares = [sound_sq(heat, material_id) for material_id in range(3)]
    phases = [mixture, mixture, mixture]
    for sweep in range(ITERS):
        pressures = [tillotson(phases[material_id], heat, material_id) for material_id in range(3)]
        fractions = [shares[material_id] * mixture / phases[material_id] for material_id in range(3)]
        mean_pressure = fractions[0] * pressures[0] + fractions[1] * pressures[1] + fractions[2] * pressures[2]
        phases = [phases[material_id] * (1.0 + 0.5 * jnp.tanh((mean_pressure - pressures[material_id]) / (phases[material_id] * squares[material_id]))) for material_id in range(3)]
        closure = shares[0] * mixture / phases[0] + shares[1] * mixture / phases[1] + shares[2] * mixture / phases[2]
        phases = [phase * closure for phase in phases]
    pressures = [tillotson(phases[material_id], heat, material_id) for material_id in range(3)]
    fractions = [shares[material_id] * mixture / phases[material_id] for material_id in range(3)]
    pressure = fractions[0] * pressures[0] + fractions[1] * pressures[1] + fractions[2] * pressures[2]
    sound = jnp.sqrt(fractions[0] * squares[0] + fractions[1] * squares[1] + fractions[2] * squares[2])
    return jnp.stack([pressure, sound])

def minmod(left_jump, right_jump):
    return 0.5 * (jnp.sign(left_jump) + jnp.sign(right_jump)) * jnp.minimum(jnp.abs(left_jump), jnp.abs(right_jump))

def face_flux(side, axis_id):
    speed = side[1 + axis_id] / smooth_pos(side[0])
    mass_flux = side[0] * speed
    moment_flux = (side[1:4] * speed[None]).at[axis_id].add(side[5])
    energy_flux = (side[4] + side[5]) * speed
    return jnp.concatenate([mass_flux[None], moment_flux, energy_flux[None]], 0)

def flux_divergence(cons_wide, sound_wide, axis_id):
    array_axis = axis_id + 1
    fields = jnp.concatenate([cons_wide, sound_wide[0:1]], 0)
    cells = fields.shape[array_axis] - 4
    jumps = lax.slice_in_dim(fields, 1, cells + 4, axis=array_axis) - lax.slice_in_dim(fields, 0, cells + 3, axis=array_axis)
    limited = minmod(lax.slice_in_dim(jumps, 0, cells + 2, axis=array_axis), lax.slice_in_dim(jumps, 1, cells + 3, axis=array_axis))
    left = lax.slice_in_dim(fields, 1, cells + 2, axis=array_axis) + 0.5 * lax.slice_in_dim(limited, 0, cells + 1, axis=array_axis)
    right = lax.slice_in_dim(fields, 2, cells + 3, axis=array_axis) - 0.5 * lax.slice_in_dim(limited, 1, cells + 2, axis=array_axis)
    signal = jnp.abs(cons_wide[1 + axis_id]) / smooth_pos(cons_wide[0]) + sound_wide[1]
    wave = jnp.maximum(lax.slice_in_dim(signal, 1, cells + 2, axis=axis_id), lax.slice_in_dim(signal, 2, cells + 3, axis=axis_id))
    flux = 0.5 * (face_flux(left, axis_id) + face_flux(right, axis_id)) - 0.5 * wave[None] * (right[:5] - left[:5])
    return lax.slice_in_dim(flux, 1, cells + 1, axis=array_axis) - lax.slice_in_dim(flux, 0, cells, axis=array_axis)

def wrap_pad(fields, array_axis):
    cells = fields.shape[array_axis]
    return jnp.concatenate([lax.slice_in_dim(fields, cells - 2, cells, axis=array_axis), fields, lax.slice_in_dim(fields, 0, 2, axis=array_axis)], array_axis)

def reference(density, momentum, energy, material, tick_counts):
    conserved = jnp.concatenate([density[None], momentum, energy[None]], 0)
    for section in range(STEPS):
        pressure_sound = state_eos(conserved, material)
        step_size = tick_counts[section].astype(jnp.float32) * TIME_UNIT
        divergence = flux_divergence(wrap_pad(conserved, 1), wrap_pad(pressure_sound, 1), 0)
        divergence = divergence + flux_divergence(wrap_pad(conserved, 2), wrap_pad(pressure_sound, 2), 1)
        divergence = divergence + flux_divergence(wrap_pad(conserved, 3), wrap_pad(pressure_sound, 3), 2)
        conserved = conserved - step_size * divergence
    return (conserved[0], conserved[1:4], conserved[4])
```

```python
import functools

import jax
import jax.numpy as jnp
from jax import lax
from jax.experimental import pallas as pl
from jax.experimental.pallas import tpu as pltpu
from jax.sharding import PartitionSpec as P

MESH = pl.DeviceIdType.MESH
STEPS = 3
ITERS = 4
RHO_REF = (1.0, 0.5, 2.7)
BULK_LIN = (1.0, 0.0, 12.0)
BULK_QUAD = (6.0, 0.0, 12.0)
COEF_LOW = (0.7, 0.4, 0.5)
COEF_HIGH = (0.15, 0.0, 1.5)
ENERGY_REF = (3.0, 1.0, 20.0)
TIME_UNIT = 0.015
ROWS = 8
LANES = 128
AXES = ("gx", "gy", "gz")


def root(value):
    return value * lax.rsqrt(value)


def smooth_pos(value):
    return 0.5 * (value + root(value * value + 0.01))


def tillotson(phase, square, mass_heat, heat_scaled, k):
    gas = COEF_LOW[k]
    if COEF_HIGH[k] != 0.0:
        gas = gas + COEF_HIGH[k] * square / (heat_scaled[k] + square)
    total = gas * mass_heat
    if BULK_LIN[k] == 0.0 and BULK_QUAD[k] == 0.0:
        return total
    quad = BULK_QUAD[k] / RHO_REF[k]
    rest = BULK_LIN[k] - BULK_QUAD[k]
    if rest == 0.0:
        return total + phase * (quad / RHO_REF[k] * phase - quad)
    eta = phase if RHO_REF[k] == 1.0 else phase * (1.0 / RHO_REF[k])
    return total + (eta - 1.0) * (quad * phase + rest)


def shares_of(mask):
    high = mask >= 4.0
    rest = jnp.where(high, mask - 4.0, mask)
    middle = rest >= 2.0
    low = jnp.where(middle, rest - 2.0, rest)
    flags = [low, jnp.where(middle, 1.0, 0.0), jnp.where(high, 1.0, 0.0)]
    count = flags[0] + flags[1] + flags[2]
    part = 1.0 / count
    return [flag * part for flag in flags]


def state_eos(fields, shares):
    mixture = smooth_pos(fields[0])
    inverse = 1.0 / mixture
    velocity = [fields[1 + d] * inverse for d in range(3)]
    heat = smooth_pos(
        fields[4] * inverse
        - 0.5 * (velocity[0] * velocity[0] + velocity[1] * velocity[1] + velocity[2] * velocity[2])
    )
    amounts = [share * mixture for share in shares]
    squares = [
        BULK_LIN[k] / RHO_REF[k] + 0.1 + (COEF_LOW[k] + COEF_HIGH[k]) * heat for k in range(3)
    ]
    soft = [1.0 / square for square in squares]
    heat_scaled = [heat * (RHO_REF[k] * RHO_REF[k] / ENERGY_REF[k]) for k in range(3)]

    def all_pressures(phases):
        return [tillotson(r, r * r, r * heat, heat_scaled, k) for k, r in enumerate(phases)]

    phases = [mixture] * 3
    parts = [inverse] * 3
    weights = shares
    opened = None
    for _ in range(ITERS):
        pressures = all_pressures(phases)
        mean = weights[0] * pressures[0] + weights[1] * pressures[1] + weights[2] * pressures[2]
        gains = [parts[k] * soft[k] for k in range(3)]
        if opened is not None:
            mean = mean * opened
            gains = [gain * opened for gain in gains]
        phases = [
            phases[k] * (2.0 + jnp.tanh((mean - pressures[k]) * gains[k])) for k in range(3)
        ]
        parts = [1.0 / phase for phase in phases]
        weights = [amounts[k] * parts[k] for k in range(3)]
        closure = weights[0] + weights[1] + weights[2]
        phases = [phase * closure for phase in phases]
        opened = 1.0 / closure
    pressures = all_pressures(phases)
    pressure = opened * (weights[0] * pressures[0] + weights[1] * pressures[1] + weights[2] * pressures[2])
    sound = root(
        opened * (weights[0] * squares[0] + weights[1] * squares[1] + weights[2] * squares[2])
    )
    return pressure, [jnp.abs(velocity[d]) + sound for d in range(3)]


def minmod(left, right):
    return jnp.maximum(jnp.minimum(left, right), 0.0) + jnp.minimum(jnp.maximum(left, right), 0.0)


def side_flux(side, d):
    speed = side[1 + d] / smooth_pos(side[0])
    out = [side[0] * speed] + [side[1 + j] * speed for j in range(3)] + [(side[4] + side[5]) * speed]
    out[1 + d] = out[1 + d] + side[5]
    return out


def cell_sides(q, before, after, d):
    halves = [0.5 * minmod(q[f] - before[f], after[f] - q[f]) for f in range(6)]
    left = [q[f] + halves[f] for f in range(6)]
    right = [q[f] - halves[f] for f in range(6)]
    return left, side_flux(left, d), right, side_flux(right, d)


def join(left, flux_left, signal_left, right, flux_right, signal_right):
    wave = jnp.maximum(signal_left, signal_right)
    return [flux_left[f] + flux_right[f] - wave * (right[f] - left[f]) for f in range(5)]


def kernel(
    density, momentum, energy, material, ticks_hbm, final,
    state, side_y, pack_z, got_x, got_y, got_z,
    mask_raw, ticks, shares, shares_x, shares_y, own_p, own_s, div,
    send_sem, recv_sem, load_sem,
):
    me = {axis: lax.axis_index(axis) for axis in AXES}
    size = {axis: lax.axis_size(axis) for axis in AXES}

    def peer(axis, way):
        n = size[axis]
        return {axis: lax.rem(me[axis] + (n - 1 if way == 0 else 1), n)}

    rows = state.shape[2]
    barrier = pltpu.get_barrier_semaphore()

    def greet(axis):
        for way in range(2):
            pl.semaphore_signal(barrier, inc=1, device_id=peer(axis, way), device_id_type=MESH)

    loads = [
        pltpu.make_async_copy(material, mask_raw, load_sem.at[0]),
        pltpu.make_async_copy(density, state.at[0, 0:1], load_sem.at[1]),
        pltpu.make_async_copy(momentum, state.at[0, 1:4], load_sem.at[2]),
        pltpu.make_async_copy(energy, state.at[0, 4:5], load_sem.at[3]),
        pltpu.make_async_copy(ticks_hbm, ticks, load_sem.at[4]),
    ]
    for load in loads:
        load.start()
    for axis in ("gz", "gx", "gy"):
        greet(axis)

    lane = lax.broadcasted_iota(jnp.int32, (ROWS, LANES), 1)
    octet = lax.div(lane, 8)
    spot = lax.rem(lane, 8)
    early = spot < 4
    lower_half = lane < LANES // 2
    at_edge = (lane < 2) | (lane >= LANES - 2)

    def gather_edges(read, count):
        packs = []
        for group in range(-(-count // 2)):
            total = None
            for f in range(group * 2, min(count, group * 2 + 2)):
                for x in range(ROWS):
                    start = 64 * (f % 2) + 8 * x
                    moved = pltpu.roll(read(f, x), (start + 4) % LANES, 1)
                    total = moved if total is None else jnp.where(octet == start // 8, moved, total)
            packs.append(total)
        return packs

    def tile(x):
        return pl.ds(x * ROWS, ROWS)

    def strided(y):
        return pl.ds(y, ROWS, stride=ROWS)

    def edge_rows(way):
        return pl.ds(0 if way == 0 else rows - 2 * ROWS, 2 * ROWS)

    def sent(step):
        return 6 if step == 0 else 5

    def rim_copy(step, a, way):
        fields = pl.ds(0, sent(step))
        if a == 0:
            src = state.at[step, fields, edge_rows(way), :]
        elif a == 1:
            src = side_y.at[step, way, fields]
        else:
            src = pack_z.at[step]
        into = (got_x, got_y, got_z)[a].at[step, 1 - way]
        return pltpu.make_async_remote_copy(
            src_ref=src,
            dst_ref=into if a == 2 else into.at[fields],
            send_sem=send_sem.at[step, a, way],
            recv_sem=recv_sem.at[step, a, 1 - way],
            device_id=peer(AXES[a], way),
            device_id_type=MESH,
        )

    def send(step, a):
        for way in range(2):
            rim_copy(step, a, way).start()

    def arrive(step, a, way):
        rim_copy(step, a, 1 - way).wait_recv()

    def stage(step):
        for way in range(2):
            for f in range(sent(step)):
                for k in range(2):
                    side_y[step, way, f, tile(k), :] = state[
                        step, f, strided(k if way == 0 else ROWS - 2 + k), :
                    ]

    def pack(step):
        packs = gather_edges(lambda f, x: state[step, f, tile(x), :], 5)
        packs[2] = jnp.where(lower_half, packs[2], pltpu.roll(mask_pack, 64, 1))
        for g in range(3):
            pack_z[step, g] = packs[g]

    for load in loads:
        load.wait()
    state[0, 5] = mask_raw[...].astype(jnp.float32)
    mask_pack = gather_edges(lambda f, x: state[0, 5, tile(x), :], 1)[0]
    pack(0)
    stage(0)
    pl.semaphore_wait(barrier, 6)
    for a in (2, 0, 1):
        send(0, a)

    for x in range(ROWS):
        for k, value in enumerate(shares_of(state[0, 5, tile(x), :])):
            shares[k, tile(x), :] = value

    def up(v):
        return pltpu.roll(v, LANES - 1, 1)

    def down(v):
        return pltpu.roll(v, 1, 1)

    def depth(q, signal):
        left, flux_left, right, flux_right = cell_sides(q, [down(v) for v in q], [up(v) for v in q], 2)
        upper = join(
            left, flux_left, signal, [up(v) for v in right], [up(v) for v in flux_right], up(signal)
        )
        return [v - down(v) for v in upper]

    def body(step):
        chunk = 2 * ROWS
        for start in range(0, rows, chunk):
            at = pl.ds(start, chunk)
            p, signals = state_eos(
                [state[step, f, at, :] for f in range(5)], [shares[k, at, :] for k in range(3)]
            )
            own_p[at, :] = p
            for d in range(3):
                own_s[d, at, :] = signals[d]

        def own(a, i):
            at = tile(i) if a == 0 else strided(i)
            return [state[step, f, at, :] for f in range(5)] + [own_p[at, :]], own_s[a, at, :]

        def face(sides, cells, i):
            left, flux_left, _, _ = sides[i]
            _, _, right, flux_right = sides[i + 1]
            return join(left, flux_left, cells[i][1], right, flux_right, cells[i + 1][1])

        def interior(a, emit):
            cells = {i: own(a, i) for i in range(ROWS)}
            sides = {
                i: cell_sides(cells[i][0], cells[i - 1][0], cells[i + 1][0], a) for i in range(1, ROWS - 1)
            }
            faces = {i: face(sides, cells, i) for i in range(1, ROWS - 2)}
            for i in range(2, ROWS - 2):
                emit(i, [faces[i][f] - faces[i - 1][f] for f in range(5)])
            return (
                {i: sides[i] for i in (1, ROWS - 2)},
                {i: faces[i] for i in (1, ROWS - 3)},
            )

        def open_shares(way, got, shares_got):
            if step == 0:
                for k, value in enumerate(shares_of(got[0, way, 5])):
                    shares_got[way, k] = value

        def border(a, way, got, shares_got, kept, emit):
            sides, faces = dict(kept[0]), dict(kept[1])
            near = (0, 1) if way == 0 else (ROWS - 2, ROWS - 1)
            cells = {i: own(a, i) for i in near}
            fields = [got[step, way, f] for f in range(5)]
            p, signals = state_eos(fields, [shares_got[way, k] for k in range(3)])
            for k in range(2):
                cells[k - 2 if way == 0 else ROWS + k] = (
                    [v[k * ROWS : (k + 1) * ROWS] for v in fields + [p]],
                    signals[a][k * ROWS : (k + 1) * ROWS],
                )
            for i in (-1, 0) if way == 0 else (ROWS - 1, ROWS):
                sides[i] = cell_sides(cells[i][0], cells[i - 1][0], cells[i + 1][0], a)
            for i in (-1, 0) if way == 0 else (ROWS - 2, ROWS - 1):
                faces[i] = face(sides, cells, i)
            for i in near:
                emit(i, [faces[i][f] - faces[i - 1][f] for f in range(5)])

        def emit_x(x, values):
            for f in range(5):
                div[0, f, tile(x), :] = values[f]

        def emit_y(y, values):
            for f in range(5):
                div[1, f, strided(y), :] = values[f]

        for x in range(ROWS):
            at = tile(x)
            values = depth([state[step, f, at, :] for f in range(5)] + [own_p[at, :]], own_s[2, at, :])
            for f in range(5):
                div[2, f, at, :] = values[f]
        edges = gather_edges(lambda f, x: own_p[tile(x), :] if f == 0 else own_s[2, tile(x), :], 2)[0]
        kept_y = interior(1, emit_y)
        kept_x = interior(0, emit_x)

        for way in (1, 0):
            arrive(step, 1, way)
        for way in (1, 0):
            open_shares(way, got_y, shares_y)
            border(1, way, got_y, shares_y, kept_y, emit_y)
        scale = ticks[step].astype(jnp.float32) * TIME_UNIT * 0.5
        for x in range(ROWS):
            at = tile(x)
            for f in range(5):
                part = div[1, f, at, :] + jnp.where(at_edge, 0.0, div[2, f, at, :])
                if 2 <= x < ROWS - 2:
                    part = part + div[0, f, at, :]
                div[2, f, at, :] = part

        arrive(step, 0, 1)
        open_shares(1, got_x, shares_x)
        border(0, 1, got_x, shares_x, kept_x, emit_x)

        for way in (1, 0):
            arrive(step, 2, way)
        arrive(step, 0, 0)
        rim_packs = [jnp.where(early, got_z[step, 0, g], got_z[step, 1, g]) for g in range(3)]

        def align(pack, f):
            return pack[f // 2] if f % 2 == 0 else pltpu.roll(pack[f // 2], LANES // 2, 1)

        rim = [align(rim_packs, f) for f in range(5)]
        p, signals = state_eos(rim, shares_of(jnp.where(lower_half, align(rim_packs, 5), 1.0)))
        outside = rim + [p, signals[2]]
        inside = [align([pack_z[step, g] for g in range(3)], f) for f in range(5)]
        inside += [edges, pltpu.roll(edges, LANES // 2, 1)]
        window = [
            jnp.where(
                lower_half,
                jnp.where(early, inside[f], outside[f]),
                pltpu.roll(jnp.where(early, outside[f], inside[f]), LANES // 2, 1),
            )
            for f in range(7)
        ]
        ends = [
            jnp.where(early, v, pltpu.roll(v, LANES // 2, 1)) for v in depth(window[:6], window[6])
        ]
        open_shares(0, got_x, shares_x)
        border(0, 0, got_x, shares_x, kept_x, emit_x)

        last = step + 1 == STEPS
        for x in (0, 1, ROWS - 2, ROWS - 1, *range(2, ROWS - 2)):
            at = tile(x)
            for f in range(5):
                end = pltpu.roll(ends[f], (LANES - 4 - 8 * x) % LANES, 1)
                total = div[2, f, at, :] + jnp.where(at_edge, end, 0.0)
                if not 2 <= x < ROWS - 2:
                    total = total + div[0, f, at, :]
                value = state[step, f, at, :] - scale * total
                if last:
                    final[f, at, :] = value
                else:
                    state[step + 1, f, at, :] = value
            if x == ROWS - 1 and not last:
                send(step + 1, 0)
        if not last:
            pack(step + 1)
            send(step + 1, 2)
            stage(step + 1)
            send(step + 1, 1)

    for step in range(STEPS):
        body(step)

    for way in range(2):
        for a in range(3):
            for step in range(STEPS):
                rim_copy(step, a, way).wait_send()


def store(final, density, momentum, energy, sem):
    stores = [
        pltpu.make_async_copy(final.at[0:1], density, sem.at[0]),
        pltpu.make_async_copy(final.at[1:4], momentum, sem.at[1]),
        pltpu.make_async_copy(final.at[4:5], energy, sem.at[2]),
    ]
    for copy in stores:
        copy.start()
    for copy in stores:
        copy.wait()


def solution(mesh):
    def per_device(density, momentum, energy, material, tick_counts):
        nx, ny, nz = density.shape
        assert (nx, ny, nz) == (ROWS, ROWS, LANES), "tile shape"
        rows = nx * ny
        f32 = jnp.float32
        vmem = pl.BlockSpec(memory_space=pltpu.VMEM)
        rim = (2 * ROWS, LANES)
        anywhere = pl.BlockSpec(memory_space=pl.ANY)
        final = pl.pallas_call(
            kernel,
            out_shape=pltpu.VMEM((5, rows, nz), f32),
            in_specs=[anywhere] * 5,
            out_specs=vmem,
            scratch_shapes=[
                pltpu.VMEM((STEPS, 6, rows, nz), f32),
                pltpu.VMEM((STEPS, 2, 6) + rim, f32),
                pltpu.VMEM((STEPS, 3, ROWS, LANES), f32),
                pltpu.VMEM((STEPS, 2, 6) + rim, f32),
                pltpu.VMEM((STEPS, 2, 6) + rim, f32),
                pltpu.VMEM((STEPS, 2, 3, ROWS, LANES), f32),
                pltpu.VMEM((rows, nz), jnp.int32),
                pltpu.SMEM((STEPS,), jnp.int32),
                pltpu.VMEM((3, rows, nz), f32),
                pltpu.VMEM((2, 3) + rim, f32),
                pltpu.VMEM((2, 3) + rim, f32),
                pltpu.VMEM((rows, nz), f32),
                pltpu.VMEM((3, rows, nz), f32),
                pltpu.VMEM((3, 5, rows, nz), f32),
                pltpu.SemaphoreType.DMA((STEPS, 3, 2)),
                pltpu.SemaphoreType.DMA((STEPS, 3, 2)),
                pltpu.SemaphoreType.DMA((5,)),
            ],
            compiler_params=pltpu.CompilerParams(collective_id=0, has_side_effects=True),
            name="hydro_steps",
        )(
            density.reshape(1, rows, nz),
            momentum.reshape(3, rows, nz),
            energy.reshape(1, rows, nz),
            material.reshape(rows, nz),
            tick_counts,
        )
        outs = pl.pallas_call(
            store,
            out_shape=tuple(jax.ShapeDtypeStruct((n, rows, nz), f32) for n in (1, 3, 1)),
            in_specs=[anywhere],
            out_specs=(anywhere,) * 3,
            scratch_shapes=[pltpu.SemaphoreType.DMA((3,))],
            compiler_params=pltpu.CompilerParams(vmem_limit_bytes=1 << 20),
            name="store_state",
        )(final)
        return (
            outs[0].reshape(nx, ny, nz),
            outs[1].reshape(3, nx, ny, nz),
            outs[2].reshape(nx, ny, nz),
        )

    placed = P("gx", "gy", "gz")
    moved = P(None, "gx", "gy", "gz")
    return jax.shard_map(
        per_device,
        mesh=mesh,
        in_specs=(placed, moved, placed, placed, P()),
        out_specs=(placed, moved, placed),
        check_vma=False,
    )
```

```python
import functools

import jax
import jax.numpy as jnp
from jax import lax
from jax.experimental import pallas as pl
from jax.experimental.pallas import tpu as pltpu
from jax.sharding import PartitionSpec as P

MESH = pl.DeviceIdType.MESH
STEPS = 3
ITERS = 4
RHO_REF = (1.0, 0.5, 2.7)
BULK_LIN = (1.0, 0.0, 12.0)
BULK_QUAD = (6.0, 0.0, 12.0)
COEF_LOW = (0.7, 0.4, 0.5)
COEF_HIGH = (0.15, 0.0, 1.5)
ENERGY_REF = (3.0, 1.0, 20.0)
TIME_UNIT = 0.015
ROWS = 8
LANES = 128
AXES = ("gx", "gy", "gz")


def root(value):
    return value * lax.rsqrt(value)


def smooth_pos(value):
    return 0.5 * (value + root(value * value + 0.01))


def tillotson(phase, square, mass_heat, heat_scaled, k):
    gas = COEF_LOW[k]
    if COEF_HIGH[k] != 0.0:
        gas = gas + COEF_HIGH[k] * square / (heat_scaled[k] + square)
    total = gas * mass_heat
    if BULK_LIN[k] == 0.0 and BULK_QUAD[k] == 0.0:
        return total
    quad = BULK_QUAD[k] / RHO_REF[k]
    rest = BULK_LIN[k] - BULK_QUAD[k]
    if rest == 0.0:
        return total + phase * (quad / RHO_REF[k] * phase - quad)
    eta = phase if RHO_REF[k] == 1.0 else phase * (1.0 / RHO_REF[k])
    return total + (eta - 1.0) * (quad * phase + rest)


def shares_of(mask):
    high = mask >= 4.0
    rest = jnp.where(high, mask - 4.0, mask)
    middle = rest >= 2.0
    low = jnp.where(middle, rest - 2.0, rest)
    flags = [low, jnp.where(middle, 1.0, 0.0), jnp.where(high, 1.0, 0.0)]
    count = flags[0] + flags[1] + flags[2]
    part = 1.0 / count
    return [flag * part for flag in flags]


def state_eos(fields, shares):
    mixture = smooth_pos(fields[0])
    inverse = 1.0 / mixture
    velocity = [fields[1 + d] * inverse for d in range(3)]
    heat = smooth_pos(
        fields[4] * inverse
        - 0.5 * (velocity[0] * velocity[0] + velocity[1] * velocity[1] + velocity[2] * velocity[2])
    )
    amounts = [share * mixture for share in shares]
    squares = [
        BULK_LIN[k] / RHO_REF[k] + 0.1 + (COEF_LOW[k] + COEF_HIGH[k]) * heat for k in range(3)
    ]
    soft = [1.0 / square for square in squares]
    heat_scaled = [heat * (RHO_REF[k] * RHO_REF[k] / ENERGY_REF[k]) for k in range(3)]

    def all_pressures(phases):
        return [tillotson(r, r * r, r * heat, heat_scaled, k) for k, r in enumerate(phases)]

    phases = [mixture] * 3
    parts = [inverse] * 3
    weights = shares
    opened = None
    for _ in range(ITERS):
        pressures = all_pressures(phases)
        mean = weights[0] * pressures[0] + weights[1] * pressures[1] + weights[2] * pressures[2]
        gains = [parts[k] * soft[k] for k in range(3)]
        if opened is not None:
            mean = mean * opened
            gains = [gain * opened for gain in gains]
        phases = [
            phases[k] * (2.0 + jnp.tanh((mean - pressures[k]) * gains[k])) for k in range(3)
        ]
        parts = [1.0 / phase for phase in phases]
        weights = [amounts[k] * parts[k] for k in range(3)]
        closure = weights[0] + weights[1] + weights[2]
        phases = [phase * closure for phase in phases]
        opened = 1.0 / closure
    pressures = all_pressures(phases)
    pressure = opened * (weights[0] * pressures[0] + weights[1] * pressures[1] + weights[2] * pressures[2])
    sound = root(
        opened * (weights[0] * squares[0] + weights[1] * squares[1] + weights[2] * squares[2])
    )
    return pressure, [jnp.abs(velocity[d]) + sound for d in range(3)]


def minmod(left, right):
    return jnp.maximum(jnp.minimum(left, right), 0.0) + jnp.minimum(jnp.maximum(left, right), 0.0)


def side_flux(side, d):
    speed = side[1 + d] / smooth_pos(side[0])
    out = [side[0] * speed] + [side[1 + j] * speed for j in range(3)] + [(side[4] + side[5]) * speed]
    out[1 + d] = out[1 + d] + side[5]
    return out


def cell_sides(q, before, after, d):
    halves = [0.5 * minmod(q[f] - before[f], after[f] - q[f]) for f in range(6)]
    left = [q[f] + halves[f] for f in range(6)]
    right = [q[f] - halves[f] for f in range(6)]
    return left, side_flux(left, d), right, side_flux(right, d)


def join(left, flux_left, signal_left, right, flux_right, signal_right):
    wave = jnp.maximum(signal_left, signal_right)
    return [flux_left[f] + flux_right[f] - wave * (right[f] - left[f]) for f in range(5)]


def kernel(
    density, momentum, energy, material, ticks_hbm, final,
    state, side_y, pack_z, got_x, got_y, got_z,
    mask_raw, ticks, shares, shares_x, shares_y, shares_z, own_p, own_s, div,
    send_sem, recv_sem, load_sem,
):
    me = {axis: lax.axis_index(axis) for axis in AXES}
    size = {axis: lax.axis_size(axis) for axis in AXES}

    def peer(axis, way):
        n = size[axis]
        return {axis: lax.rem(me[axis] + (n - 1 if way == 0 else 1), n)}

    rows = state.shape[2]
    barrier = pltpu.get_barrier_semaphore()

    def greet(axis):
        for way in range(2):
            pl.semaphore_signal(barrier, inc=1, device_id=peer(axis, way), device_id_type=MESH)

    loads = [
        pltpu.make_async_copy(material, mask_raw, load_sem.at[0]),
        pltpu.make_async_copy(density, state.at[0, 0:1], load_sem.at[1]),
        pltpu.make_async_copy(momentum, state.at[0, 1:4], load_sem.at[2]),
        pltpu.make_async_copy(energy, state.at[0, 4:5], load_sem.at[3]),
        pltpu.make_async_copy(ticks_hbm, ticks, load_sem.at[4]),
    ]
    for load in loads:
        load.start()
    for axis in ("gz", "gx", "gy"):
        greet(axis)

    lane = lax.broadcasted_iota(jnp.int32, (ROWS, LANES), 1)
    octet = lax.div(lane, 8)
    half = LANES // 2
    lower_half = lane < half
    is_out = lax.div(lane, half) + lax.div(lax.rem(lane, 8), 4) == 1
    at_low = lane < 2
    at_edge = at_low | (lane >= LANES - 2)

    def edge_pack(read):
        total = None
        for x in range(ROWS):
            for start in (8 * x, half + 8 * x):
                moved = pltpu.roll(read(x), start + 4, 1)
                total = moved if total is None else jnp.where(octet == start // 8, moved, total)
        return total

    def tile(x):
        return pl.ds(x * ROWS, ROWS)

    def strided(y):
        return pl.ds(y, ROWS, stride=ROWS)

    def edge_rows(way):
        return pl.ds(0 if way == 0 else rows - 2 * ROWS, 2 * ROWS)

    def sent(step):
        return 6 if step == 0 else 5

    def rim_copy(step, a, way):
        fields = pl.ds(0, sent(step))
        if a == 0:
            src = state.at[step, fields, edge_rows(way), :]
        elif a == 1:
            src = side_y.at[step, way, fields]
        else:
            src = pack_z.at[step, fields]
        into = (got_x, got_y, got_z)[a].at[step, 1 - way]
        return pltpu.make_async_remote_copy(
            src_ref=src,
            dst_ref=into.at[fields],
            send_sem=send_sem.at[step, a, way],
            recv_sem=recv_sem.at[step, a, 1 - way],
            device_id=peer(AXES[a], way),
            device_id_type=MESH,
        )

    def send(step, a):
        for way in range(2):
            rim_copy(step, a, way).start()

    def arrive(step, a, way):
        rim_copy(step, a, 1 - way).wait_recv()

    def stage(step):
        for way in range(2):
            for f in range(sent(step)):
                for k in range(2):
                    side_y[step, way, f, tile(k), :] = state[
                        step, f, strided(k if way == 0 else ROWS - 2 + k), :
                    ]

    def pack(step):
        for f in range(sent(step)):
            pack_z[step, f] = edge_pack(lambda x: state[step, f, tile(x), :])

    for load in loads:
        load.wait()
    state[0, 5] = mask_raw[...].astype(jnp.float32)
    pack(0)
    stage(0)
    pl.semaphore_wait(barrier, 6)
    for a in (2, 0, 1):
        send(0, a)

    for x in range(ROWS):
        for k, value in enumerate(shares_of(state[0, 5, tile(x), :])):
            shares[k, tile(x), :] = value

    def up(v):
        return pltpu.roll(v, LANES - 1, 1)

    def down(v):
        return pltpu.roll(v, 1, 1)

    def depth(q, signal):
        left, flux_left, right, flux_right = cell_sides(q, [down(v) for v in q], [up(v) for v in q], 2)
        upper = join(
            left, flux_left, signal, [up(v) for v in right], [up(v) for v in flux_right], up(signal)
        )
        return [v - down(v) for v in upper]

    def rim_depth(q, signal):
        below = [down(v) for v in q]
        above = [up(v) for v in q]
        step_down = [q[f] - below[f] for f in range(6)]
        step_up = [above[f] - q[f] for f in range(6)]
        far_down = [below[f] - pltpu.roll(q[f], 2, 1) for f in range(6)]
        far_up = [pltpu.roll(q[f], LANES - 2, 1) - above[f] for f in range(6)]
        halves = [0.5 * minmod(step_down[f], step_up[f]) for f in range(6)]
        halves_below = [0.5 * minmod(far_down[f], step_down[f]) for f in range(6)]
        halves_above = [0.5 * minmod(step_up[f], far_up[f]) for f in range(6)]

        def face(left, signal_left, right, signal_right):
            return join(left, side_flux(left, 2), signal_left, right, side_flux(right, 2), signal_right)

        upper = face(
            [q[f] + halves[f] for f in range(6)], signal,
            [above[f] - halves_above[f] for f in range(6)], up(signal),
        )
        lower = face(
            [below[f] + halves_below[f] for f in range(6)], down(signal),
            [q[f] - halves[f] for f in range(6)], signal,
        )
        return [upper[f] - lower[f] for f in range(5)]

    def body(step):
        chunk = 2 * ROWS
        for start in range(0, rows, chunk):
            at = pl.ds(start, chunk)
            p, signals = state_eos(
                [state[step, f, at, :] for f in range(5)], [shares[k, at, :] for k in range(3)]
            )
            own_p[at, :] = p
            for d in range(3):
                own_s[d, at, :] = signals[d]

        def own(a, i):
            at = tile(i) if a == 0 else strided(i)
            return [state[step, f, at, :] for f in range(5)] + [own_p[at, :]], own_s[a, at, :]

        def face(sides, cells, i):
            left, flux_left, _, _ = sides[i]
            _, _, right, flux_right = sides[i + 1]
            return join(left, flux_left, cells[i][1], right, flux_right, cells[i + 1][1])

        def interior(a, emit):
            cells = {i: own(a, i) for i in range(ROWS)}
            sides = {
                i: cell_sides(cells[i][0], cells[i - 1][0], cells[i + 1][0], a) for i in range(1, ROWS - 1)
            }
            faces = {i: face(sides, cells, i) for i in range(1, ROWS - 2)}
            for i in range(2, ROWS - 2):
                emit(i, [faces[i][f] - faces[i - 1][f] for f in range(5)])
            return (
                {i: sides[i] for i in (1, ROWS - 2)},
                {i: faces[i] for i in (1, ROWS - 3)},
            )

        def open_shares(way, got, shares_got):
            if step == 0:
                for k, value in enumerate(shares_of(got[0, way, 5])):
                    shares_got[way, k] = value

        def border(a, way, got, shares_got, kept, emit):
            sides, faces = dict(kept[0]), dict(kept[1])
            near = (0, 1) if way == 0 else (ROWS - 2, ROWS - 1)
            cells = {i: own(a, i) for i in near}
            fields = [got[step, way, f] for f in range(5)]
            p, signals = state_eos(fields, [shares_got[way, k] for k in range(3)])
            for k in range(2):
                cells[k - 2 if way == 0 else ROWS + k] = (
                    [v[k * ROWS : (k + 1) * ROWS] for v in fields + [p]],
                    signals[a][k * ROWS : (k + 1) * ROWS],
                )
            for i in (-1, 0) if way == 0 else (ROWS - 1, ROWS):
                sides[i] = cell_sides(cells[i][0], cells[i - 1][0], cells[i + 1][0], a)
            for i in (-1, 0) if way == 0 else (ROWS - 2, ROWS - 1):
                faces[i] = face(sides, cells, i)
            for i in near:
                emit(i, [faces[i][f] - faces[i - 1][f] for f in range(5)])

        def emit_x(x, values):
            for f in range(5):
                div[0, f, tile(x), :] = values[f]

        def emit_y(y, values):
            for f in range(5):
                div[1, f, strided(y), :] = values[f]

        for x in range(ROWS):
            at = tile(x)
            values = depth([state[step, f, at, :] for f in range(5)] + [own_p[at, :]], own_s[2, at, :])
            for f in range(5):
                div[2, f, at, :] = values[f]
        edge_p = edge_pack(lambda x: own_p[tile(x), :])
        edge_s = edge_pack(lambda x: own_s[2, tile(x), :])
        kept_y = interior(1, emit_y)
        kept_x = interior(0, emit_x)

        for way in (1, 0):
            arrive(step, 1, way)
        for way in (1, 0):
            open_shares(way, got_y, shares_y)
            border(1, way, got_y, shares_y, kept_y, emit_y)
        scale = ticks[step].astype(jnp.float32) * TIME_UNIT * 0.5
        for x in range(ROWS):
            at = tile(x)
            for f in range(5):
                part = div[1, f, at, :] + jnp.where(at_edge, 0.0, div[2, f, at, :])
                if 2 <= x < ROWS - 2:
                    part = part + div[0, f, at, :]
                div[2, f, at, :] = part

        arrive(step, 0, 1)
        open_shares(1, got_x, shares_x)
        border(0, 1, got_x, shares_x, kept_x, emit_x)

        for way in (1, 0):
            arrive(step, 2, way)
        arrive(step, 0, 0)
        outside = [
            jnp.where(lower_half, got_z[step, 1, f], got_z[step, 0, f]) for f in range(sent(step))
        ]
        if step == 0:
            for k, value in enumerate(shares_of(outside.pop())):
                shares_z[k] = value
        p, signals = state_eos(outside, [shares_z[k] for k in range(3)])
        window = [jnp.where(is_out, outside[f], pack_z[step, f]) for f in range(5)]
        ends = rim_depth(window + [jnp.where(is_out, p, edge_p)], jnp.where(is_out, signals[2], edge_s))
        open_shares(0, got_x, shares_x)
        border(0, 0, got_x, shares_x, kept_x, emit_x)

        last = step + 1 == STEPS
        for x in (0, 1, ROWS - 2, ROWS - 1, *range(2, ROWS - 2)):
            at = tile(x)
            for f in range(5):
                end = jnp.where(
                    at_low,
                    pltpu.roll(ends[f], (half - 4 - 8 * x) % LANES, 1),
                    pltpu.roll(ends[f], LANES - 4 - 8 * x, 1),
                )
                total = div[2, f, at, :] + jnp.where(at_edge, end, 0.0)
                if not 2 <= x < ROWS - 2:
                    total = total + div[0, f, at, :]
                value = state[step, f, at, :] - scale * total
                if last:
                    final[f, at, :] = value
                else:
                    state[step + 1, f, at, :] = value
            if x == ROWS - 1 and not last:
                send(step + 1, 0)
        if not last:
            pack(step + 1)
            send(step + 1, 2)
            stage(step + 1)
            send(step + 1, 1)

    for step in range(STEPS):
        body(step)

    for way in range(2):
        for a in range(3):
            for step in range(STEPS):
                rim_copy(step, a, way).wait_send()


def store(final, density, momentum, energy, sem):
    stores = [
        pltpu.make_async_copy(final.at[0:1], density, sem.at[0]),
        pltpu.make_async_copy(final.at[1:4], momentum, sem.at[1]),
        pltpu.make_async_copy(final.at[4:5], energy, sem.at[2]),
    ]
    for copy in stores:
        copy.start()
    for copy in stores:
        copy.wait()


def solution(mesh):
    def per_device(density, momentum, energy, material, tick_counts):
        nx, ny, nz = density.shape
        assert (nx, ny, nz) == (ROWS, ROWS, LANES), "tile shape"
        rows = nx * ny
        f32 = jnp.float32
        vmem = pl.BlockSpec(memory_space=pltpu.VMEM)
        rim = (2 * ROWS, LANES)
        anywhere = pl.BlockSpec(memory_space=pl.ANY)
        final = pl.pallas_call(
            kernel,
            out_shape=pltpu.VMEM((5, rows, nz), f32),
            in_specs=[anywhere] * 5,
            out_specs=vmem,
            scratch_shapes=[
                pltpu.VMEM((STEPS, 6, rows, nz), f32),
                pltpu.VMEM((STEPS, 2, 6) + rim, f32),
                pltpu.VMEM((STEPS, 6, ROWS, LANES), f32),
                pltpu.VMEM((STEPS, 2, 6) + rim, f32),
                pltpu.VMEM((STEPS, 2, 6) + rim, f32),
                pltpu.VMEM((STEPS, 2, 6, ROWS, LANES), f32),
                pltpu.VMEM((rows, nz), jnp.int32),
                pltpu.SMEM((STEPS,), jnp.int32),
                pltpu.VMEM((3, rows, nz), f32),
                pltpu.VMEM((2, 3) + rim, f32),
                pltpu.VMEM((2, 3) + rim, f32),
                pltpu.VMEM((3, ROWS, LANES), f32),
                pltpu.VMEM((rows, nz), f32),
                pltpu.VMEM((3, rows, nz), f32),
                pltpu.VMEM((3, 5, rows, nz), f32),
                pltpu.SemaphoreType.DMA((STEPS, 3, 2)),
                pltpu.SemaphoreType.DMA((STEPS, 3, 2)),
                pltpu.SemaphoreType.DMA((5,)),
            ],
            compiler_params=pltpu.CompilerParams(collective_id=0, has_side_effects=True),
            name="hydro_steps",
        )(
            density.reshape(1, rows, nz),
            momentum.reshape(3, rows, nz),
            energy.reshape(1, rows, nz),
            material.reshape(rows, nz),
            tick_counts,
        )
        outs = pl.pallas_call(
            store,
            out_shape=tuple(jax.ShapeDtypeStruct((n, rows, nz), f32) for n in (1, 3, 1)),
            in_specs=[anywhere],
            out_specs=(anywhere,) * 3,
            scratch_shapes=[pltpu.SemaphoreType.DMA((3,))],
            compiler_params=pltpu.CompilerParams(vmem_limit_bytes=1 << 20),
            name="store_state",
        )(final)
        return (
            outs[0].reshape(nx, ny, nz),
            outs[1].reshape(3, nx, ny, nz),
            outs[2].reshape(nx, ny, nz),
        )

    placed = P("gx", "gy", "gz")
    moved = P(None, "gx", "gy", "gz")
    return jax.shard_map(
        per_device,
        mesh=mesh,
        in_specs=(placed, moved, placed, placed, P()),
        out_specs=(placed, moved, placed),
        check_vma=False,
    )
```

```python
import functools

import jax
import jax.numpy as jnp
from jax import lax
from jax.experimental import pallas as pl
from jax.experimental.pallas import tpu as pltpu
from jax.sharding import PartitionSpec as P

MESH = pl.DeviceIdType.MESH
STEPS = 3
ITERS = 4
RHO_REF = (1.0, 0.5, 2.7)
BULK_LIN = (1.0, 0.0, 12.0)
BULK_QUAD = (6.0, 0.0, 12.0)
COEF_LOW = (0.7, 0.4, 0.5)
COEF_HIGH = (0.15, 0.0, 1.5)
ENERGY_REF = (3.0, 1.0, 20.0)
TIME_UNIT = 0.015
ROWS = 8
LANES = 128
AXES = ("gx", "gy", "gz")


def root(value):
    return value * lax.rsqrt(value)


def smooth_pos(value):
    return 0.5 * (value + root(value * value + 0.01))


def tillotson(phase, square, mass_heat, heat_scaled, k):
    gas = COEF_LOW[k]
    if COEF_HIGH[k] != 0.0:
        gas = gas + COEF_HIGH[k] * square / (heat_scaled[k] + square)
    total = gas * mass_heat
    if BULK_LIN[k] == 0.0 and BULK_QUAD[k] == 0.0:
        return total
    quad = BULK_QUAD[k] / RHO_REF[k]
    rest = BULK_LIN[k] - BULK_QUAD[k]
    if rest == 0.0:
        return total + phase * (quad / RHO_REF[k] * phase - quad)
    eta = phase if RHO_REF[k] == 1.0 else phase * (1.0 / RHO_REF[k])
    return total + (eta - 1.0) * (quad * phase + rest)


def shares_of(mask):
    high = mask >= 4.0
    rest = jnp.where(high, mask - 4.0, mask)
    middle = rest >= 2.0
    low = jnp.where(middle, rest - 2.0, rest)
    flags = [low, jnp.where(middle, 1.0, 0.0), jnp.where(high, 1.0, 0.0)]
    count = flags[0] + flags[1] + flags[2]
    part = 1.0 / count
    return [flag * part for flag in flags]


def state_eos(fields, shares):
    mixture = smooth_pos(fields[0])
    inverse = 1.0 / mixture
    velocity = [fields[1 + d] * inverse for d in range(3)]
    heat = smooth_pos(
        fields[4] * inverse
        - 0.5 * (velocity[0] * velocity[0] + velocity[1] * velocity[1] + velocity[2] * velocity[2])
    )
    amounts = [share * mixture for share in shares]
    squares = [
        BULK_LIN[k] / RHO_REF[k] + 0.1 + (COEF_LOW[k] + COEF_HIGH[k]) * heat for k in range(3)
    ]
    soft = [1.0 / square for square in squares]
    heat_scaled = [heat * (RHO_REF[k] * RHO_REF[k] / ENERGY_REF[k]) for k in range(3)]

    def all_pressures(phases):
        return [tillotson(r, r * r, r * heat, heat_scaled, k) for k, r in enumerate(phases)]

    phases = [mixture] * 3
    parts = [inverse] * 3
    weights = shares
    opened = None
    for _ in range(ITERS):
        pressures = all_pressures(phases)
        mean = weights[0] * pressures[0] + weights[1] * pressures[1] + weights[2] * pressures[2]
        gains = [parts[k] * soft[k] for k in range(3)]
        if opened is not None:
            mean = mean * opened
            gains = [gain * opened for gain in gains]
        phases = [
            phases[k] * (2.0 + jnp.tanh((mean - pressures[k]) * gains[k])) for k in range(3)
        ]
        parts = [1.0 / phase for phase in phases]
        weights = [amounts[k] * parts[k] for k in range(3)]
        closure = weights[0] + weights[1] + weights[2]
        phases = [phase * closure for phase in phases]
        opened = 1.0 / closure
    pressures = all_pressures(phases)
    pressure = opened * (weights[0] * pressures[0] + weights[1] * pressures[1] + weights[2] * pressures[2])
    sound = root(
        opened * (weights[0] * squares[0] + weights[1] * squares[1] + weights[2] * squares[2])
    )
    return pressure, [jnp.abs(velocity[d]) + sound for d in range(3)]


def minmod(left, right):
    return jnp.maximum(jnp.minimum(left, right), 0.0) + jnp.minimum(jnp.maximum(left, right), 0.0)


def side_flux(side, d):
    speed = side[1 + d] / smooth_pos(side[0])
    out = [side[0] * speed] + [side[1 + j] * speed for j in range(3)] + [(side[4] + side[5]) * speed]
    out[1 + d] = out[1 + d] + side[5]
    return out


def cell_sides(q, before, after, d):
    halves = [0.5 * minmod(q[f] - before[f], after[f] - q[f]) for f in range(6)]
    left = [q[f] + halves[f] for f in range(6)]
    right = [q[f] - halves[f] for f in range(6)]
    return left, side_flux(left, d), right, side_flux(right, d)


def join(left, flux_left, signal_left, right, flux_right, signal_right):
    wave = jnp.maximum(signal_left, signal_right)
    return [flux_left[f] + flux_right[f] - wave * (right[f] - left[f]) for f in range(5)]


def kernel(
    density, momentum, energy, material, ticks_hbm, final,
    state, side_y, pack_z, got_x, got_y, got_z,
    mask_raw, ticks, shares, shares_x, shares_y, shares_z, own_p, own_s, div,
    send_sem, recv_sem, load_sem,
):
    me = {axis: lax.axis_index(axis) for axis in AXES}
    size = {axis: lax.axis_size(axis) for axis in AXES}

    def peer(axis, way):
        n = size[axis]
        return {axis: lax.rem(me[axis] + (n - 1 if way == 0 else 1), n)}

    rows = state.shape[2]
    barrier = pltpu.get_barrier_semaphore()

    def greet(axis):
        for way in range(2):
            pl.semaphore_signal(barrier, inc=1, device_id=peer(axis, way), device_id_type=MESH)

    loads = [
        pltpu.make_async_copy(material, mask_raw, load_sem.at[0]),
        pltpu.make_async_copy(density, state.at[0, 0:1], load_sem.at[1]),
        pltpu.make_async_copy(momentum, state.at[0, 1:4], load_sem.at[2]),
        pltpu.make_async_copy(energy, state.at[0, 4:5], load_sem.at[3]),
        pltpu.make_async_copy(ticks_hbm, ticks, load_sem.at[4]),
    ]
    for load in loads:
        load.start()
    for axis in ("gz", "gx", "gy"):
        greet(axis)

    lane = lax.broadcasted_iota(jnp.int32, (ROWS, LANES), 1)
    octet = lax.div(lane, 8)
    half = LANES // 2
    lower_half = lane < half
    spot = lax.rem(lane, 8)
    is_out = lax.div(lane, half) + lax.div(spot, 4) == 1
    inner = (spot >= 2) & (spot < 6)
    at_edge = (lane < 2) | (lane >= LANES - 2)

    def place(read, picked, starts, total=None):
        for x in picked:
            for start in starts:
                moved = pltpu.roll(read(x), (start + 8 * x + 4) % LANES, 1)
                total = moved if total is None else jnp.where(octet == start // 8 + x, moved, total)
        return total

    def edge_pack(read, picked=range(ROWS)):
        total = place(read, picked, (0,))
        return jnp.where(lower_half, total, pltpu.roll(total, half, 1))

    def tile(x):
        return pl.ds(x * ROWS, ROWS)

    def strided(y):
        return pl.ds(y, ROWS, stride=ROWS)

    def edge_rows(way):
        return pl.ds(0 if way == 0 else rows - 2 * ROWS, 2 * ROWS)

    def sent(step):
        return 6 if step == 0 else 5

    def rim_copy(step, a, way):
        fields = pl.ds(0, sent(step))
        if a == 0:
            src = state.at[step, fields, edge_rows(way), :]
        elif a == 1:
            src = side_y.at[step, way, fields]
        else:
            src = pack_z.at[step, fields]
        into = (got_x, got_y, got_z)[a].at[step, 1 - way]
        return pltpu.make_async_remote_copy(
            src_ref=src,
            dst_ref=into.at[fields],
            send_sem=send_sem.at[a, way],
            recv_sem=recv_sem.at[step % 2, a, 1 - way],
            device_id=peer(AXES[a], way),
            device_id_type=MESH,
        )

    def send(step, a):
        for way in range(2):
            rim_copy(step, a, way).start()

    def arrive(step, a, way):
        rim_copy(step, a, 1 - way).wait_recv()

    def stage(step):
        for way in range(2):
            for f in range(sent(step)):
                for k in range(2):
                    side_y[step, way, f, tile(k), :] = state[
                        step, f, strided(k if way == 0 else ROWS - 2 + k), :
                    ]

    for load in loads:
        load.wait()
    state[0, 5] = mask_raw[...].astype(jnp.float32)
    for f in range(6):
        pack_z[0, f] = edge_pack(lambda x: state[0, f, tile(x), :])
    stage(0)
    pl.semaphore_wait(barrier, 6)
    for a in (2, 0, 1):
        send(0, a)

    for x in range(ROWS):
        for k, value in enumerate(shares_of(state[0, 5, tile(x), :])):
            shares[k, tile(x), :] = value

    def up(v):
        return pltpu.roll(v, LANES - 1, 1)

    def down(v):
        return pltpu.roll(v, 1, 1)

    def depth(q, signal):
        left, flux_left, right, flux_right = cell_sides(q, [down(v) for v in q], [up(v) for v in q], 2)
        upper = join(
            left, flux_left, signal, [up(v) for v in right], [up(v) for v in flux_right], up(signal)
        )
        return [v - down(v) for v in upper]

    def rim_depth(q, signal):
        below = [down(v) for v in q]
        above = [up(v) for v in q]
        step_down = [q[f] - below[f] for f in range(6)]
        step_up = [above[f] - q[f] for f in range(6)]
        far_down = [below[f] - pltpu.roll(q[f], 2, 1) for f in range(6)]
        far_up = [pltpu.roll(q[f], LANES - 2, 1) - above[f] for f in range(6)]
        halves = [0.5 * minmod(step_down[f], step_up[f]) for f in range(6)]
        halves_below = [0.5 * minmod(far_down[f], step_down[f]) for f in range(6)]
        halves_above = [0.5 * minmod(step_up[f], far_up[f]) for f in range(6)]

        def face(left, signal_left, right, signal_right):
            return join(left, side_flux(left, 2), signal_left, right, side_flux(right, 2), signal_right)

        upper = face(
            [q[f] + halves[f] for f in range(6)], signal,
            [above[f] - halves_above[f] for f in range(6)], up(signal),
        )
        lower = face(
            [below[f] + halves_below[f] for f in range(6)], down(signal),
            [q[f] - halves[f] for f in range(6)], signal,
        )
        return [upper[f] - lower[f] for f in range(5)]

    def body(step):
        chunk = 2 * ROWS
        for start in range(0, rows, chunk):
            at = pl.ds(start, chunk)
            p, signals = state_eos(
                [state[step, f, at, :] for f in range(5)], [shares[k, at, :] for k in range(3)]
            )
            own_p[at, :] = p
            for d in range(3):
                own_s[d, at, :] = signals[d]

        def own(a, i):
            at = tile(i) if a == 0 else strided(i)
            return [state[step, f, at, :] for f in range(5)] + [own_p[at, :]], own_s[a, at, :]

        def face(sides, cells, i):
            left, flux_left, _, _ = sides[i]
            _, _, right, flux_right = sides[i + 1]
            return join(left, flux_left, cells[i][1], right, flux_right, cells[i + 1][1])

        def interior(a, emit):
            cells = {i: own(a, i) for i in range(ROWS)}
            sides = {
                i: cell_sides(cells[i][0], cells[i - 1][0], cells[i + 1][0], a) for i in range(1, ROWS - 1)
            }
            faces = {i: face(sides, cells, i) for i in range(1, ROWS - 2)}
            for i in range(2, ROWS - 2):
                emit(i, [faces[i][f] - faces[i - 1][f] for f in range(5)])
            return (
                {i: sides[i] for i in (1, ROWS - 2)},
                {i: faces[i] for i in (1, ROWS - 3)},
            )

        def open_shares(way, got, shares_got):
            if step == 0:
                for k, value in enumerate(shares_of(got[0, way, 5])):
                    shares_got[way, k] = value

        def border(a, way, got, shares_got, kept, emit):
            sides, faces = dict(kept[0]), dict(kept[1])
            near = (0, 1) if way == 0 else (ROWS - 2, ROWS - 1)
            cells = {i: own(a, i) for i in near}
            fields = [got[step, way, f] for f in range(5)]
            p, signals = state_eos(fields, [shares_got[way, k] for k in range(3)])
            for k in range(2):
                cells[k - 2 if way == 0 else ROWS + k] = (
                    [v[k * ROWS : (k + 1) * ROWS] for v in fields + [p]],
                    signals[a][k * ROWS : (k + 1) * ROWS],
                )
            for i in (-1, 0) if way == 0 else (ROWS - 1, ROWS):
                sides[i] = cell_sides(cells[i][0], cells[i - 1][0], cells[i + 1][0], a)
            for i in (-1, 0) if way == 0 else (ROWS - 2, ROWS - 1):
                faces[i] = face(sides, cells, i)
            for i in near:
                emit(i, [faces[i][f] - faces[i - 1][f] for f in range(5)])

        def emit_x(x, values):
            for f in range(5):
                div[0, f, tile(x), :] = values[f]

        def emit_y(y, values):
            for f in range(5):
                div[1, f, strided(y), :] = values[f]

        for x in range(ROWS):
            at = tile(x)
            values = depth([state[step, f, at, :] for f in range(5)] + [own_p[at, :]], own_s[2, at, :])
            for f in range(5):
                div[2, f, at, :] = values[f]
        edge_p = edge_pack(lambda x: own_p[tile(x), :])
        edge_s = edge_pack(lambda x: own_s[2, tile(x), :])
        kept_y = interior(1, emit_y)
        kept_x = interior(0, emit_x)

        for a in (2, 0, 1):
            for way in range(2):
                rim_copy(step, a, way).wait_send()
        for way in (1, 0):
            arrive(step, 1, way)
        for way in (1, 0):
            open_shares(way, got_y, shares_y)
            border(1, way, got_y, shares_y, kept_y, emit_y)
        scale = ticks[step].astype(jnp.float32) * TIME_UNIT * 0.5
        last = step + 1 == STEPS
        middle = range(2, ROWS - 2)

        def settle(picked):
            for x in picked:
                at = tile(x)
                for f in range(5):
                    total = div[0, f, at, :] + div[1, f, at, :] + jnp.where(at_edge, 0.0, div[2, f, at, :])
                    div[2, f, at, :] = state[step, f, at, :] - scale * total

        def settled(f):
            return lambda x: div[2, f, tile(x), :]

        settle(middle)
        if not last:
            packs = [place(settled(f), middle, (0,)) for f in range(5)]

        arrive(step, 0, 1)
        open_shares(1, got_x, shares_x)
        border(0, 1, got_x, shares_x, kept_x, emit_x)
        settle((ROWS - 2, ROWS - 1))
        if not last:
            packs = [place(settled(f), (ROWS - 2, ROWS - 1), (0,), packs[f]) for f in range(5)]
            packs = [jnp.where(lower_half, v, pltpu.roll(v, half, 1)) for v in packs]

        for way in (1, 0):
            arrive(step, 2, way)
        arrive(step, 0, 0)
        outside = [
            jnp.where(lower_half, got_z[step, 1, f], got_z[step, 0, f]) for f in range(sent(step))
        ]
        if step == 0:
            for k, value in enumerate(shares_of(outside.pop())):
                shares_z[k] = value
        p, signals = state_eos(outside, [shares_z[k] for k in range(3)])
        window = [jnp.where(is_out, outside[f], pack_z[step, f]) for f in range(5)]
        ends = rim_depth(window + [jnp.where(is_out, p, edge_p)], jnp.where(is_out, signals[2], edge_s))
        open_shares(0, got_x, shares_x)
        border(0, 0, got_x, shares_x, kept_x, emit_x)

        settle((0, 1))
        ends = [
            jnp.where(inner, scale * jnp.where(is_out, pltpu.roll(v, half, 1), v), 0.0) for v in ends
        ]
        if not last:
            for f in range(5):
                pack_z[step + 1, f] = place(settled(f), (0, 1), (0, half), packs[f]) - ends[f]
            send(step + 1, 2)
        for x in (0, 1, ROWS - 2, ROWS - 1, *middle):
            at = tile(x)
            for f in range(5):
                end = pltpu.roll(ends[f], (LANES - 4 - 8 * x) % LANES, 1)
                value = div[2, f, at, :] - jnp.where(at_edge, end, 0.0)
                if last:
                    final[f, at, :] = value
                else:
                    state[step + 1, f, at, :] = value
            if x == ROWS - 1 and not last:
                send(step + 1, 0)
        if not last:
            stage(step + 1)
            send(step + 1, 1)

    for step in range(STEPS):
        body(step)


def store(final, density, momentum, energy, sem):
    stores = [
        pltpu.make_async_copy(final.at[0:1], density, sem.at[0]),
        pltpu.make_async_copy(final.at[1:4], momentum, sem.at[1]),
        pltpu.make_async_copy(final.at[4:5], energy, sem.at[2]),
    ]
    for copy in stores:
        copy.start()
    for copy in stores:
        copy.wait()


def solution(mesh):
    def per_device(density, momentum, energy, material, tick_counts):
        nx, ny, nz = density.shape
        assert (nx, ny, nz) == (ROWS, ROWS, LANES), "tile shape"
        rows = nx * ny
        f32 = jnp.float32
        vmem = pl.BlockSpec(memory_space=pltpu.VMEM)
        rim = (2 * ROWS, LANES)
        anywhere = pl.BlockSpec(memory_space=pl.ANY)
        final = pl.pallas_call(
            kernel,
            out_shape=pltpu.VMEM((5, rows, nz), f32),
            in_specs=[anywhere] * 5,
            out_specs=vmem,
            scratch_shapes=[
                pltpu.VMEM((STEPS, 6, rows, nz), f32),
                pltpu.VMEM((STEPS, 2, 6) + rim, f32),
                pltpu.VMEM((STEPS, 6, ROWS, LANES), f32),
                pltpu.VMEM((STEPS, 2, 6) + rim, f32),
                pltpu.VMEM((STEPS, 2, 6) + rim, f32),
                pltpu.VMEM((STEPS, 2, 6, ROWS, LANES), f32),
                pltpu.VMEM((rows, nz), jnp.int32),
                pltpu.SMEM((STEPS,), jnp.int32),
                pltpu.VMEM((3, rows, nz), f32),
                pltpu.VMEM((2, 3) + rim, f32),
                pltpu.VMEM((2, 3) + rim, f32),
                pltpu.VMEM((3, ROWS, LANES), f32),
                pltpu.VMEM((rows, nz), f32),
                pltpu.VMEM((3, rows, nz), f32),
                pltpu.VMEM((3, 5, rows, nz), f32),
                pltpu.SemaphoreType.DMA((3, 2)),
                pltpu.SemaphoreType.DMA((2, 3, 2)),
                pltpu.SemaphoreType.DMA((5,)),
            ],
            compiler_params=pltpu.CompilerParams(collective_id=0, has_side_effects=True),
            name="hydro_steps",
        )(
            density.reshape(1, rows, nz),
            momentum.reshape(3, rows, nz),
            energy.reshape(1, rows, nz),
            material.reshape(rows, nz),
            tick_counts,
        )
        outs = pl.pallas_call(
            store,
            out_shape=tuple(jax.ShapeDtypeStruct((n, rows, nz), f32) for n in (1, 3, 1)),
            in_specs=[anywhere],
            out_specs=(anywhere,) * 3,
            scratch_shapes=[pltpu.SemaphoreType.DMA((3,))],
            compiler_params=pltpu.CompilerParams(vmem_limit_bytes=1 << 20),
            name="store_state",
        )(final)
        return (
            outs[0].reshape(nx, ny, nz),
            outs[1].reshape(3, nx, ny, nz),
            outs[2].reshape(nx, ny, nz),
        )

    placed = P("gx", "gy", "gz")
    moved = P(None, "gx", "gy", "gz")
    return jax.shard_map(
        per_device,
        mesh=mesh,
        in_specs=(placed, moved, placed, placed, P()),
        out_specs=(placed, moved, placed),
        check_vma=False,
    )
```
